32 devices in a mesh: seq: 16 (over z, y, x), ch: 2 (over core).
Axes of the slice: x: 2, y: 2, z: 4, core: 2. Of those that a mesh axis runs over, the one named last changes fastest.
Arguments:
- signal: float32 [4096, 256], P('seq', 'ch'), may hold values from -6 to 6
- decay_rate: float32 [256, 64], P('ch'), may hold values from 0.00024414062 to 0.05
- frequency: float32 [256, 64], P('ch'), may hold values from 0.00024414062 to 0.0625
- coeff_real: float32 [256, 64], P('ch'), may hold values from -0.5 to 0.5
- coeff_imag: float32 [256, 64], P('ch'), may hold values from -0.5 to 0.5
- skip_weight: float32 [256], P('ch'), may hold values from 0.3 to 3
- norm_gain: float32 [256], P('ch'), may hold values from 0.1 to 1.9
Outputs:
- normed: float32 [4096, 256], P('seq', 'ch')
The draws below stay inside these ranges and needn't reach their ends.
All inputs are finite; a program needn't handle non-finite values.
Results may differ from the reference program's by a relative error of at most 0.00021.
Values sent between devices are 32-bit elements; how exact they have to be, the bound alone decides.
A program may use at most 64 MiB of HBM per device.

```python
import math
import jax
import jax.numpy as jnp
from jax import lax

D = 256
MODES = 64
LENGTH = 4096


def block_scale(own_key, extent, cuts, low, top_value):
    loudness = 1.0
    for position, blocks in cuts:
        heights = jax.random.uniform(jax.random.fold_in(jax.random.fold_in(own_key, 6), position), (blocks,), jnp.float32, low / len(cuts), top_value / len(cuts))
        loudness = loudness * jnp.repeat(jnp.exp(heights), extent[position] // blocks).reshape((-1,) + (1,) * (len(extent) - 1 - position))
    return loudness


def noise(rng, extent, deviation, limit, pieces=(), kind=jnp.bfloat16):
    entries = jax.random.normal(rng, extent, jnp.float32) * deviation
    if len(pieces) > 0:
        entries = block_scale(rng, extent, pieces, -0.22, 0.18) * entries
    return jnp.clip(entries, min=-limit, max=limit).astype(kind)


def setup_inputs(seed: int = 0) -> dict:
    seeds = jax.random.split(jax.random.key(seed), 8)
    return {
        "signal": noise(seeds[0], (LENGTH, D), 1.0, 6.0, ((0, 16), (1, 2)), jnp.float32),
        "decay_rate": jnp.clip(jnp.exp(math.log(0.05) - 5.322034 * jax.random.uniform(seeds[1], (D, MODES), jnp.float32) ** block_scale(seeds[1], (D, MODES), ((0, 2),), -0.2, 0.2)), 0.00024414062, 0.05),
        "frequency": jnp.clip(jnp.exp(math.log(0.0625) - 5.5451774 * jax.random.uniform(seeds[2], (D, MODES), jnp.float32) ** block_scale(seeds[2], (D, MODES), ((0, 2),), -0.2, 0.2)), 0.00024414062, 0.0625),
        "coeff_real": noise(seeds[3], (D, MODES), 0.09, 0.5, ((0, 2),), jnp.float32),
        "coeff_imag": noise(seeds[4], (D, MODES), 0.09, 0.5, ((0, 2),), jnp.float32),
        "skip_weight": jnp.clip(jnp.exp(math.log(3.0) - 2.3025851 * jax.random.uniform(seeds[5], (D,), jnp.float32) ** block_scale(seeds[5], (D,), ((0, 2),), -0.2, 0.2)), 0.3, 3.0),
        "norm_gain": jnp.clip(1.0 + 0.18 * jax.random.normal(seeds[6], (D,), jnp.float32), 0.1, 1.9),
    }


def reference(signal, decay_rate, frequency, coeff_real, coeff_imag, skip_weight, norm_gain):
    block_size = 128
    num_blocks = LENGTH // block_size
    starts = jnp.arange(num_blocks, dtype=jnp.float32) * block_size
    offsets = jnp.arange(block_size, dtype=jnp.float32)

    def channel(packed):
        column, decay_row, freq_row, real_row, imag_row = packed
        factor = 2.0 * jnp.sqrt(decay_row)
        lead_mag = factor[None, :] * jnp.exp(-decay_row[None, :] * starts[:, None])
        lead_phase = freq_row[None, :] * starts[:, None]
        lead_real = lead_mag * (real_row[None, :] * jnp.cos(lead_phase) - imag_row[None, :] * jnp.sin(lead_phase))
        lead_imag = lead_mag * (real_row[None, :] * jnp.sin(lead_phase) + imag_row[None, :] * jnp.cos(lead_phase))
        tail_mag = jnp.exp(-decay_row[:, None] * offsets[None, :])
        tail_phase = freq_row[:, None] * offsets[None, :]
        kernel = jnp.dot(lead_real, tail_mag * jnp.cos(tail_phase), precision=lax.Precision.HIGHEST, preferred_element_type=jnp.float32)
        kernel = kernel - jnp.dot(lead_imag, tail_mag * jnp.sin(tail_phase), precision=lax.Precision.HIGHEST, preferred_element_type=jnp.float32)
        kernel = kernel.reshape(LENGTH)
        spectrum = jnp.fft.rfft(column, n=2 * LENGTH) * jnp.fft.rfft(kernel, n=2 * LENGTH)
        return jnp.fft.irfft(spectrum, n=2 * LENGTH)[:LENGTH]
    convolved = lax.map(channel, (signal.T, decay_rate, frequency, coeff_real, coeff_imag)).T
    summed = convolved + skip_weight[None, :] * signal
    token_mean = lax.optimization_barrier(jnp.mean(summed, axis=1, keepdims=True))
    token_power = lax.optimization_barrier(jnp.mean(summed * summed, axis=1, keepdims=True))
    token_var = token_power - token_mean * token_mean
    return (summed - token_mean) * lax.rsqrt(token_var + 1e-05) * norm_gain[None, :]
```

```python
import functools
import math

import jax
import jax.numpy as jnp
from jax import lax
from jax.experimental import pallas as pl
from jax.experimental.pallas import tpu as pltpu
from jax.sharding import PartitionSpec as P

MESH = pl.DeviceIdType.MESH
CHUNK = 128
NT = (((1,), (1,)), ((), ()))
NN = (((1,), (0,)), ((), ()))


def split(value):
    high = value.astype(jnp.bfloat16)
    low = (value - high.astype(jnp.float32)).astype(jnp.bfloat16)
    return high, low


def product(value, high_w, low_w, dims):
    rows = value.shape[0]
    high, low = split(value)
    both = lax.dot_general(
        jnp.concatenate([high, low], axis=0), high_w, dims, preferred_element_type=jnp.float32
    )
    rest = lax.dot_general(high, low_w, dims, preferred_element_type=jnp.float32)
    return both[:rows] + (both[rows:] + rest)


def kernel_body(
    shards,
    halves_of_ch,
    sig_hbm,
    decay_hbm,
    freq_hbm,
    real_hbm,
    imag_hbm,
    skip_ref,
    gain_ref,
    out_ref,
    x_ref,
    params,
    send_a,
    recv_a,
    send_b,
    recv_b,
    skipped,
    in_high,
    in_low,
    out_high,
    out_low,
    near,
    ends_real,
    ends_imag,
    carried,
    mine,
    theirs,
    load_sems,
    send_sems,
    recv_sems,
    own_sems,
    pair_sems,
):
    me = lax.axis_index("seq")
    my_ch = lax.axis_index("ch")
    rows, chans = x_ref.shape
    per_dev = chans // shards
    modes = decay_hbm.shape[1]
    parts = rows // CHUNK
    total = shards * parts

    barrier = pltpu.get_barrier_semaphore()
    for hop in range(1, shards):
        pl.semaphore_signal(
            barrier,
            inc=1,
            device_id={"seq": lax.rem(me + hop, shards), "ch": my_ch},
            device_id_type=MESH,
        )
    for hop in range(1, halves_of_ch):
        pl.semaphore_signal(
            barrier,
            inc=1,
            device_id={"seq": me, "ch": lax.rem(my_ch + hop, halves_of_ch)},
            device_id_type=MESH,
        )

    loads = [pltpu.make_async_copy(sig_hbm, x_ref, load_sems.at[0])]
    for i, ref in enumerate((decay_hbm, freq_hbm, real_hbm, imag_hbm)):
        loads.append(pltpu.make_async_copy(ref, params.at[i], load_sems.at[i + 1]))
    for copy in loads:
        copy.start()
    loads[0].wait()
    turned = x_ref[...].T
    for i in range(shards):
        for part in range(parts):
            send_a[i, part] = turned[
                i * per_dev : (i + 1) * per_dev, part * CHUNK : (part + 1) * CHUNK
            ]

    pl.semaphore_wait(barrier, shards - 1 + halves_of_ch - 1)

    def exchange(source, landing, phase):
        own = pltpu.make_async_copy(source.at[me], landing.at[me], own_sems.at[phase])
        copies = []
        for hop in range(shards - 1, 0, -1):
            target = lax.rem(me + hop, shards)
            copies.append(
                pltpu.make_async_remote_copy(
                    src_ref=source.at[target],
                    dst_ref=landing.at[me],
                    send_sem=send_sems.at[phase, hop],
                    recv_sem=recv_sems.at[phase, hop],
                    device_id={"seq": target, "ch": my_ch},
                    device_id_type=MESH,
                )
            )
        for copy in copies:
            copy.start()
        own.start()
        return own, copies

    own_a, copies_a = exchange(send_a, recv_a, 0)

    skipped[...] = (x_ref[...] * skip_ref[...]).T
    for copy in loads[1:]:
        copy.wait()
    first = me * per_dev
    doubled = []
    for i in range(4):
        row = params[i, pl.ds(first, per_dev), :]
        doubled.append(jnp.concatenate([row, row], axis=1))
    decay, freq, real, imag = doubled
    amplitude = 2.0 * jnp.sqrt(decay)
    real, imag = amplitude * real, amplitude * imag
    lanes = 2 * modes

    def is_imag(count):
        return lax.broadcasted_iota(jnp.int32, (count, lanes), 1) >= modes

    upper = is_imag(per_dev)
    step_real = jnp.exp(-decay) * jnp.cos(freq)
    step_imag = jnp.exp(-decay) * jnp.sin(freq)
    lead_real = real * step_real - imag * step_imag
    lead_imag = real * step_imag + imag * step_real
    lead_real = jnp.where(upper, -lead_real, lead_real)
    weights = jnp.where(upper, -imag, real)
    far_mag = jnp.exp(-decay * CHUNK)
    far_real = far_mag * jnp.cos(freq * CHUNK)
    far_imag = far_mag * jnp.sin(freq * CHUNK)
    far_imag = jnp.where(upper, -far_imag, far_imag)

    groups = CHUNK // 8
    ahead = lax.broadcasted_iota(jnp.int32, (8, lanes), 0).astype(jnp.float32)
    starts = 8.0 * lax.broadcasted_iota(jnp.int32, (groups, lanes), 0).astype(jnp.float32)
    row_id = lax.broadcasted_iota(jnp.int32, (CHUNK, CHUNK), 0)
    col_id = lax.broadcasted_iota(jnp.int32, (CHUNK, CHUNK), 1)
    causal = col_id >= row_id
    quarter = jnp.where(is_imag(8), 0.5 * math.pi, 0.0)

    for c in range(per_dev):
        d_row, f_row = decay[c : c + 1], freq[c : c + 1]
        inner = jnp.exp(-d_row * ahead) * jnp.cos(f_row * ahead - quarter)
        back = 7.0 - ahead
        inner_back = jnp.exp(-d_row * back) * jnp.cos(f_row * back - quarter)
        inner_turned = pltpu.roll(inner, modes, 1)
        inner_back_turned = pltpu.roll(inner_back, modes, 1)
        outer_mag = jnp.exp(-d_row * starts)
        outer_real = outer_mag * jnp.cos(f_row * starts)
        outer_imag = outer_mag * jnp.sin(f_row * starts)
        outer_imag = jnp.where(is_imag(groups), outer_imag, -outer_imag)
        forward, backward = [], []
        for g in range(groups):
            turn_r, turn_i = outer_real[g : g + 1], outer_imag[g : g + 1]
            forward.append(turn_r * inner + turn_i * inner_turned)
            back_r = outer_real[groups - 1 - g : groups - g]
            back_i = outer_imag[groups - 1 - g : groups - g]
            backward.append(back_r * inner_back + back_i * inner_back_turned)
        high, low = split(jnp.concatenate(forward, axis=0))
        out_high[c] = high
        out_low[c] = low
        taps = product(
            jnp.broadcast_to(weights[c : c + 1], (16, lanes)), high, low, NT
        )[0:1]
        spread = pltpu.roll(
            jnp.broadcast_to(taps, (CHUNK, CHUNK)), 0, 1, stride=1, stride_axis=0
        )
        high, low = split(jnp.where(causal, spread, 0.0))
        in_high[c, :, 0:CHUNK] = high
        in_low[c, :, 0:CHUNK] = low
        high, low = split(jnp.concatenate(backward, axis=0))
        in_high[c, :, CHUNK:] = high
        in_low[c, :, CHUNK:] = low

    own_a.wait()
    for copy in copies_a:
        copy.wait_recv()

    strided = per_dev % 8 == 0

    def take(c):
        if strided:
            flat = recv_a.reshape(total * per_dev, CHUNK)
            return flat[pl.ds(c, total, stride=per_dev), :]
        return recv_a[:, :, c, :].reshape(total, CHUNK)

    def put(c, value):
        if strided:
            flat = send_b.reshape(total * per_dev, CHUNK)
            flat[pl.ds(c, total, stride=per_dev), :] = value
        else:
            send_b[:, :, c, :] = value.reshape(shards, parts, CHUNK)

    for c in range(per_dev):
        both = product(take(c), in_high[c], in_low[c], NN)
        near[c] = both[:, :CHUNK]
        ends = both[:, CHUNK:]
        ends_real[pl.ds(c * total, total), :] = ends
        ends_imag[pl.ds(c * total, total), :] = pltpu.roll(ends, modes, 1)

    state_r = jnp.zeros((per_dev, lanes), jnp.float32)
    state_i = jnp.zeros((per_dev, lanes), jnp.float32)

    def advance(shard, state):
        state_r, state_i = state
        for part in range(parts):
            at = pl.ds(shard * parts + part, per_dev, stride=total)
            carried[at, :] = lead_real * state_r - lead_imag * state_i
            next_r = far_real * state_r - far_imag * state_i + ends_real[at, :]
            state_i = far_real * state_i + far_imag * state_r + ends_imag[at, :]
            state_r = next_r
        return state_r, state_i

    if shards <= 16:
        for shard in range(shards):
            state_r, state_i = advance(shard, (state_r, state_i))
    else:
        lax.fori_loop(0, shards, advance, (state_r, state_i))

    for c in range(per_dev):
        state = carried[pl.ds(c * total, total), :]
        value = near[c] + product(state, out_high[c], out_low[c], NT)
        put(c, value)

    own_b, copies_b = exchange(send_b, recv_b, 1)
    own_b.wait()
    for copy in copies_b:
        copy.wait_recv()

    for i in range(shards):
        at = pl.ds(i * per_dev, per_dev)
        for part in range(parts):
            cols = pl.ds(part * CHUNK, CHUNK)
            skipped[at, cols] = recv_b[i, part] + skipped[at, cols]
    summed = skipped[...]
    mine[0:1, :] = jnp.sum(summed, axis=0, keepdims=True)
    mine[1:2, :] = jnp.sum(summed * summed, axis=0, keepdims=True)
    pairs = []
    for hop in range(1, halves_of_ch):
        pairs.append(
            pltpu.make_async_remote_copy(
                src_ref=mine,
                dst_ref=theirs.at[hop - 1],
                send_sem=pair_sems.at[0, hop],
                recv_sem=pair_sems.at[1, hop],
                device_id={"seq": me, "ch": lax.rem(my_ch + hop, halves_of_ch)},
                device_id_type=MESH,
            )
        )
    for copy in pairs:
        copy.start()
    for copy in copies_a + copies_b:
        copy.wait_send()
    for copy in pairs:
        copy.wait()
    sums = mine[...]
    for hop in range(1, halves_of_ch):
        sums = sums + theirs[hop - 1]
    means = sums / (chans * halves_of_ch)
    token_mean = means[0:1]
    token_var = means[1:2] - token_mean * token_mean
    scaled = (summed - token_mean) * lax.rsqrt(token_var + 1e-05)
    out_ref[...] = scaled.T * gain_ref[...]


def on_device(signal, decay_rate, frequency, coeff_real, coeff_imag, skip_weight, norm_gain):
    rows, chans = signal.shape
    shards = lax.axis_size("seq")
    halves_of_ch = lax.axis_size("ch")
    modes = decay_rate.shape[1]
    per_dev = chans // shards
    total = rows // CHUNK * shards
    lanes = 2 * modes
    f32, bf16 = jnp.float32, jnp.bfloat16
    anywhere = pl.BlockSpec(memory_space=pl.ANY)
    vmem = pl.BlockSpec(memory_space=pltpu.VMEM)
    return pl.pallas_call(
        functools.partial(kernel_body, shards, halves_of_ch),
        out_shape=jax.ShapeDtypeStruct((rows, chans), f32),
        in_specs=[anywhere] * 5 + [vmem] * 2,
        out_specs=vmem,
        scratch_shapes=[
            pltpu.VMEM((rows, chans), f32),
            pltpu.VMEM((4, chans, modes), f32),
            pltpu.VMEM((shards, rows // CHUNK, per_dev, CHUNK), f32),
            pltpu.VMEM((shards, rows // CHUNK, per_dev, CHUNK), f32),
            pltpu.VMEM((shards, rows // CHUNK, per_dev, CHUNK), f32),
            pltpu.VMEM((shards, rows // CHUNK, per_dev, CHUNK), f32),
            pltpu.VMEM((chans, rows), f32),
            pltpu.VMEM((per_dev, CHUNK, CHUNK + lanes), bf16),
            pltpu.VMEM((per_dev, CHUNK, CHUNK + lanes), bf16),
            pltpu.VMEM((per_dev, CHUNK, lanes), bf16),
            pltpu.VMEM((per_dev, CHUNK, lanes), bf16),
            pltpu.VMEM((per_dev, total, CHUNK), f32),
            pltpu.VMEM((per_dev * total, lanes), f32),
            pltpu.VMEM((per_dev * total, lanes), f32),
            pltpu.VMEM((per_dev * total, lanes), f32),
            pltpu.VMEM((2, rows), f32),
            pltpu.VMEM((max(halves_of_ch - 1, 1), 2, rows), f32),
            pltpu.SemaphoreType.DMA((5,)),
            pltpu.SemaphoreType.DMA((2, shards)),
            pltpu.SemaphoreType.DMA((2, shards)),
            pltpu.SemaphoreType.DMA((2,)),
            pltpu.SemaphoreType.DMA((2, halves_of_ch)),
        ],
        compiler_params=pltpu.CompilerParams(collective_id=0, has_side_effects=True),
        name="modal_conv",
    )(
        signal,
        decay_rate,
        frequency,
        coeff_real,
        coeff_imag,
        skip_weight.reshape(1, chans),
        norm_gain.reshape(1, chans),
    )


def solution(mesh):
    placed = (
        P("seq", "ch"),
        P("ch", None),
        P("ch", None),
        P("ch", None),
        P("ch", None),
        P("ch"),
        P("ch"),
    )
    return jax.shard_map(
        on_device, mesh=mesh, in_specs=placed, out_specs=P("seq", "ch"), check_vma=False
    )
```

```python
import functools
import math

import jax
import jax.numpy as jnp
from jax import lax
from jax.experimental import pallas as pl
from jax.experimental.pallas import tpu as pltpu
from jax.sharding import PartitionSpec as P

MESH = pl.DeviceIdType.MESH
CHUNK = 128
NT = (((1,), (1,)), ((), ()))
NN = (((1,), (0,)), ((), ()))


def split(value):
    high = value.astype(jnp.bfloat16)
    low = (value - high.astype(jnp.float32)).astype(jnp.bfloat16)
    return high, low


def product(value, high_w, low_w, dims):
    rows = value.shape[0]
    high, low = split(value)
    both = lax.dot_general(
        jnp.concatenate([high, low], axis=0), high_w, dims, preferred_element_type=jnp.float32
    )
    rest = lax.dot_general(high, low_w, dims, preferred_element_type=jnp.float32)
    return both[:rows] + (both[rows:] + rest)


def kernel_body(
    shards,
    halves_of_ch,
    sig_hbm,
    decay_hbm,
    freq_hbm,
    real_hbm,
    imag_hbm,
    skip_ref,
    out_ref,
    x_ref,
    params,
    send_a,
    recv_a,
    send_b,
    recv_b,
    sums_to,
    sums_from,
    in_high,
    in_low,
    out_high,
    out_low,
    near,
    ends_real,
    ends_imag,
    carried,
    owned,
    load_sems,
    send_sems,
    recv_sems,
    own_sems,
    pair_sems,
):
    me = lax.axis_index("seq")
    my_ch = lax.axis_index("ch")
    rows, chans = x_ref.shape
    per_dev = chans // shards
    modes = decay_hbm.shape[0]
    parts = rows // CHUNK
    total = shards * parts

    barrier = pltpu.get_barrier_semaphore()
    for hop in range(1, shards):
        pl.semaphore_signal(
            barrier,
            inc=1,
            device_id={"seq": lax.rem(me + hop, shards), "ch": my_ch},
            device_id_type=MESH,
        )
    for side in range(1, halves_of_ch):
        for hop in range(shards):
            pl.semaphore_signal(
                barrier,
                inc=1,
                device_id={
                    "seq": lax.rem(me + hop, shards),
                    "ch": lax.rem(my_ch + side, halves_of_ch),
                },
                device_id_type=MESH,
            )

    loads = [pltpu.make_async_copy(sig_hbm, x_ref, load_sems.at[0])]
    for i, ref in enumerate((decay_hbm, freq_hbm, real_hbm, imag_hbm)):
        loads.append(pltpu.make_async_copy(ref, params.at[i], load_sems.at[i + 1]))
    for copy in loads:
        copy.start()
    loads[0].wait()
    turned = x_ref[...].T
    for i in range(shards):
        for part in range(parts):
            send_a[i, part] = turned[
                i * per_dev : (i + 1) * per_dev, part * CHUNK : (part + 1) * CHUNK
            ]

    pl.semaphore_wait(barrier, shards * halves_of_ch - 1)

    def exchange(source, landing, phase):
        own = pltpu.make_async_copy(source.at[me], landing.at[me], own_sems.at[phase])
        copies = []
        for hop in range(shards - 1, 0, -1):
            target = lax.rem(me + hop, shards)
            copies.append(
                pltpu.make_async_remote_copy(
                    src_ref=source.at[target],
                    dst_ref=landing.at[me],
                    send_sem=send_sems.at[phase, hop],
                    recv_sem=recv_sems.at[phase, hop],
                    device_id={"seq": target, "ch": my_ch},
                    device_id_type=MESH,
                )
            )
        for copy in copies:
            copy.start()
        own.start()
        return own, copies

    own_a, copies_a = exchange(send_a, recv_a, 0)

    for copy in loads[1:]:
        copy.wait()
    for i in range(4):
        owned[i] = jnp.concatenate([params[i], params[i]], axis=0).T
    owned[4] = jnp.broadcast_to(skip_ref[...], (2 * modes, chans)).T
    mine = pl.ds(me * per_dev, per_dev)
    decay, freq, real, imag, skip = [owned[i, mine, :] for i in range(5)]
    amplitude = 2.0 * jnp.sqrt(decay)
    real, imag = amplitude * real, amplitude * imag
    lanes = 2 * modes

    def is_imag(count):
        return lax.broadcasted_iota(jnp.int32, (count, lanes), 1) >= modes

    upper = is_imag(per_dev)
    step_real = jnp.exp(-decay) * jnp.cos(freq)
    step_imag = jnp.exp(-decay) * jnp.sin(freq)
    lead_real = real * step_real - imag * step_imag
    lead_imag = real * step_imag + imag * step_real
    lead_real = jnp.where(upper, -lead_real, lead_real)
    weights = jnp.where(upper, -imag, real)
    far_mag = jnp.exp(-decay * CHUNK)
    far_real = far_mag * jnp.cos(freq * CHUNK)
    far_imag = far_mag * jnp.sin(freq * CHUNK)
    far_imag = jnp.where(upper, -far_imag, far_imag)

    groups = CHUNK // 8
    ahead = lax.broadcasted_iota(jnp.int32, (8, lanes), 0).astype(jnp.float32)
    starts = 8.0 * lax.broadcasted_iota(jnp.int32, (groups, lanes), 0).astype(jnp.float32)
    row_id = lax.broadcasted_iota(jnp.int32, (CHUNK, CHUNK), 0)
    col_id = lax.broadcasted_iota(jnp.int32, (CHUNK, CHUNK), 1)
    causal = col_id >= row_id
    quarter = jnp.where(is_imag(8), 0.5 * math.pi, 0.0)

    for c in range(per_dev):
        d_row, f_row = decay[c : c + 1], freq[c : c + 1]
        inner = jnp.exp(-d_row * ahead) * jnp.cos(f_row * ahead - quarter)
        back = 7.0 - ahead
        inner_back = jnp.exp(-d_row * back) * jnp.cos(f_row * back - quarter)
        inner_turned = pltpu.roll(inner, modes, 1)
        inner_back_turned = pltpu.roll(inner_back, modes, 1)
        outer_mag = jnp.exp(-d_row * starts)
        outer_real = outer_mag * jnp.cos(f_row * starts)
        outer_imag = outer_mag * jnp.sin(f_row * starts)
        outer_imag = jnp.where(is_imag(groups), outer_imag, -outer_imag)
        forward, backward = [], []
        for g in range(groups):
            turn_r, turn_i = outer_real[g : g + 1], outer_imag[g : g + 1]
            forward.append(turn_r * inner + turn_i * inner_turned)
            back_r = outer_real[groups - 1 - g : groups - g]
            back_i = outer_imag[groups - 1 - g : groups - g]
            backward.append(back_r * inner_back + back_i * inner_back_turned)
        high, low = split(jnp.concatenate(forward, axis=0))
        out_high[c] = high
        out_low[c] = low
        taps = product(
            jnp.broadcast_to(weights[c : c + 1], (16, lanes)), high, low, NT
        )[0:1]
        spread = pltpu.roll(
            jnp.broadcast_to(taps, (CHUNK, CHUNK)), 0, 1, stride=1, stride_axis=0
        )
        high, low = split(jnp.where(causal, spread, 0.0))
        in_high[c, :, 0:CHUNK] = high
        in_low[c, :, 0:CHUNK] = low
        high, low = split(jnp.concatenate(backward, axis=0))
        in_high[c, :, CHUNK:] = high
        in_low[c, :, CHUNK:] = low

    own_a.wait()
    for copy in copies_a:
        copy.wait_recv()

    strided = per_dev % 8 == 0

    def take(c):
        if strided:
            flat = recv_a.reshape(total * per_dev, CHUNK)
            return flat[pl.ds(c, total, stride=per_dev), :]
        return recv_a[:, :, c, :].reshape(total, CHUNK)

    def put(c, value):
        if strided:
            flat = send_b.reshape(total * per_dev, CHUNK)
            flat[pl.ds(c, total, stride=per_dev), :] = value
        else:
            send_b[:, :, c, :] = value.reshape(shards, parts, CHUNK)

    for c in range(per_dev):
        signal = take(c)
        both = product(signal, in_high[c], in_low[c], NN)
        near[c] = both[:, :CHUNK] + skip[c : c + 1] * signal
        ends = both[:, CHUNK:]
        ends_real[pl.ds(c * total, total), :] = ends
        ends_imag[pl.ds(c * total, total), :] = pltpu.roll(ends, modes, 1)

    state_r = jnp.zeros((per_dev, lanes), jnp.float32)
    state_i = jnp.zeros((per_dev, lanes), jnp.float32)

    def advance(shard, state):
        state_r, state_i = state
        for part in range(parts):
            at = pl.ds(shard * parts + part, per_dev, stride=total)
            carried[at, :] = lead_real * state_r - lead_imag * state_i
            next_r = far_real * state_r - far_imag * state_i + ends_real[at, :]
            state_i = far_real * state_i + far_imag * state_r + ends_imag[at, :]
            state_r = next_r
        return state_r, state_i

    if shards <= 16:
        for shard in range(shards):
            state_r, state_i = advance(shard, (state_r, state_i))
    else:
        lax.fori_loop(0, shards, advance, (state_r, state_i))

    total_sum = jnp.zeros((total, CHUNK), jnp.float32)
    total_square = jnp.zeros((total, CHUNK), jnp.float32)
    for c in range(per_dev):
        state = carried[pl.ds(c * total, total), :]
        value = near[c] + product(state, out_high[c], out_low[c], NT)
        total_sum = total_sum + value
        total_square = total_square + value * value
        put(c, value)

    for shard in range(shards):
        rows_of = slice(shard * parts, (shard + 1) * parts)
        sums_to[shard, 0:parts] = total_sum[rows_of]
        sums_to[shard, parts : 2 * parts] = total_square[rows_of]

    own_b, copies_b = exchange(send_b, recv_b, 1)
    sums_copies = []
    for side in range(1, halves_of_ch):
        for hop in range(shards - 1, -1, -1):
            target = lax.rem(me + hop, shards)
            sums_copies.append(
                pltpu.make_async_remote_copy(
                    src_ref=sums_to.at[target],
                    dst_ref=sums_from.at[side - 1, me],
                    send_sem=pair_sems.at[0, side - 1, hop],
                    recv_sem=pair_sems.at[1, side - 1, hop],
                    device_id={"seq": target, "ch": lax.rem(my_ch + side, halves_of_ch)},
                    device_id_type=MESH,
                )
            )
    for copy in sums_copies:
        copy.start()
    own_b.wait()
    for copy in copies_b:
        copy.wait_recv()
    own_sums, own_squares, blocks = [], [], []
    for part in range(parts):
        block = jnp.concatenate([recv_b[i, part] for i in range(shards)], axis=0)
        blocks.append(block)
        own_sums.append(jnp.sum(block, axis=0, keepdims=True))
        own_squares.append(jnp.sum(block * block, axis=0, keepdims=True))
    sums = jnp.concatenate(own_sums + own_squares, axis=0)
    for copy in sums_copies:
        copy.wait_recv()
    for side in range(halves_of_ch - 1):
        for shard in range(shards):
            sums = sums + sums_from[side, shard]
    means = sums / (chans * halves_of_ch)
    for part in range(parts):
        token_mean = means[part : part + 1]
        token_var = means[parts + part : parts + part + 1] - token_mean * token_mean
        scaled = (blocks[part] - token_mean) * lax.rsqrt(token_var + 1e-05)
        out_ref[part * CHUNK : (part + 1) * CHUNK, :] = scaled.T
    for copy in copies_a + copies_b + sums_copies:
        copy.wait_send()


def on_device(signal, decay_rate, frequency, coeff_real, coeff_imag, skip_weight, norm_gain):
    rows, chans = signal.shape
    shards = lax.axis_size("seq")
    halves_of_ch = lax.axis_size("ch")
    modes = decay_rate.shape[1]
    per_dev = chans // shards
    parts = rows // CHUNK
    total = parts * shards
    lanes = 2 * modes
    f32, bf16 = jnp.float32, jnp.bfloat16
    anywhere = pl.BlockSpec(memory_space=pl.ANY)
    vmem = pl.BlockSpec(memory_space=pltpu.VMEM)
    normed = pl.pallas_call(
        functools.partial(kernel_body, shards, halves_of_ch),
        out_shape=jax.ShapeDtypeStruct((rows, chans), f32),
        in_specs=[anywhere] * 5 + [vmem],
        out_specs=vmem,
        scratch_shapes=[
            pltpu.VMEM((rows, chans), f32),
            pltpu.VMEM((4, modes, chans), f32),
            pltpu.VMEM((shards, rows // CHUNK, per_dev, CHUNK), f32),
            pltpu.VMEM((shards, rows // CHUNK, per_dev, CHUNK), f32),
            pltpu.VMEM((shards, rows // CHUNK, per_dev, CHUNK), f32),
            pltpu.VMEM((shards, rows // CHUNK, per_dev, CHUNK), f32),
            pltpu.VMEM((shards, 2 * parts, CHUNK), f32),
            pltpu.VMEM((max(halves_of_ch - 1, 1), shards, 2 * parts, CHUNK), f32),
            pltpu.VMEM((per_dev, CHUNK, CHUNK + lanes), bf16),
            pltpu.VMEM((per_dev, CHUNK, CHUNK + lanes), bf16),
            pltpu.VMEM((per_dev, CHUNK, lanes), bf16),
            pltpu.VMEM((per_dev, CHUNK, lanes), bf16),
            pltpu.VMEM((per_dev, total, CHUNK), f32),
            pltpu.VMEM((per_dev * total, lanes), f32),
            pltpu.VMEM((per_dev * total, lanes), f32),
            pltpu.VMEM((per_dev * total, lanes), f32),
            pltpu.VMEM((5, chans, lanes), f32),
            pltpu.SemaphoreType.DMA((5,)),
            pltpu.SemaphoreType.DMA((2, shards)),
            pltpu.SemaphoreType.DMA((2, shards)),
            pltpu.SemaphoreType.DMA((2,)),
            pltpu.SemaphoreType.DMA((2, max(halves_of_ch - 1, 1), shards)),
        ],
        compiler_params=pltpu.CompilerParams(collective_id=0, has_side_effects=True),
        name="modal_conv",
    )(
        signal,
        decay_rate.T,
        frequency.T,
        coeff_real.T,
        coeff_imag.T,
        skip_weight.reshape(1, chans),
    )
    return normed * norm_gain[None, :]


def solution(mesh):
    placed = (
        P("seq", "ch"),
        P("ch", None),
        P("ch", None),
        P("ch", None),
        P("ch", None),
        P("ch"),
        P("ch"),
    )
    return jax.shard_map(
        on_device, mesh=mesh, in_specs=placed, out_specs=P("seq", "ch"), check_vma=False
    )
```

```python
import functools
import math

import jax
import jax.numpy as jnp
from jax import lax
from jax.experimental import pallas as pl
from jax.experimental.pallas import tpu as pltpu
from jax.sharding import PartitionSpec as P

MESH = pl.DeviceIdType.MESH
CHUNK = 128
NT = (((1,), (1,)), ((), ()))
NN = (((1,), (0,)), ((), ()))


def split(value):
    high = value.astype(jnp.bfloat16)
    low = (value - high.astype(jnp.float32)).astype(jnp.bfloat16)
    return high, low


def product(value, high_w, low_w, dims):
    rows = value.shape[0]
    high, low = split(value)
    both = lax.dot_general(
        jnp.concatenate([high, low], axis=0), high_w, dims, preferred_element_type=jnp.float32
    )
    rest = lax.dot_general(high, low_w, dims, preferred_element_type=jnp.float32)
    return both[:rows] + (both[rows:] + rest)


def kernel_body(
    shards,
    halves_of_ch,
    sig_hbm,
    decay_hbm,
    freq_hbm,
    real_hbm,
    imag_hbm,
    skip_ref,
    out_ref,
    x_ref,
    params,
    send_a,
    recv_a,
    send_b,
    recv_b,
    sums_to,
    sums_from,
    in_high,
    in_low,
    out_high,
    out_low,
    near,
    ends_real,
    ends_imag,
    carried,
    owned,
    load_sems,
    send_sems,
    recv_sems,
    own_sems,
    pair_sems,
):
    me = lax.axis_index("seq")
    my_ch = lax.axis_index("ch")
    rows, chans = x_ref.shape
    per_dev = chans // shards
    modes = decay_hbm.shape[0]
    parts = rows // CHUNK
    total = shards * parts

    barrier = pltpu.get_barrier_semaphore()
    for hop in range(1, shards):
        pl.semaphore_signal(
            barrier,
            inc=1,
            device_id={"seq": lax.rem(me + hop, shards), "ch": my_ch},
            device_id_type=MESH,
        )
    for side in range(1, halves_of_ch):
        for hop in range(shards):
            pl.semaphore_signal(
                barrier,
                inc=1,
                device_id={
                    "seq": lax.rem(me + hop, shards),
                    "ch": lax.rem(my_ch + side, halves_of_ch),
                },
                device_id_type=MESH,
            )

    loads = [pltpu.make_async_copy(sig_hbm, x_ref, load_sems.at[0])]
    for i, ref in enumerate((decay_hbm, freq_hbm, real_hbm, imag_hbm)):
        loads.append(pltpu.make_async_copy(ref, params.at[i], load_sems.at[i + 1]))
    for copy in loads:
        copy.start()
    loads[0].wait()
    turned = x_ref[...].T
    for i in range(shards):
        for part in range(parts):
            send_a[i, part] = turned[
                i * per_dev : (i + 1) * per_dev, part * CHUNK : (part + 1) * CHUNK
            ]

    pl.semaphore_wait(barrier, shards * halves_of_ch - 1)

    def exchange(source, landing, phase):
        own = pltpu.make_async_copy(source.at[me], landing.at[me], own_sems.at[phase])
        copies = []
        for hop in range(shards - 1, 0, -1):
            target = lax.rem(me + hop, shards)
            copies.append(
                pltpu.make_async_remote_copy(
                    src_ref=source.at[target],
                    dst_ref=landing.at[me],
                    send_sem=send_sems.at[phase],
                    recv_sem=recv_sems.at[phase],
                    device_id={"seq": target, "ch": my_ch},
                    device_id_type=MESH,
                )
            )
        for copy in copies:
            copy.start()
        own.start()
        others = landing.at[pl.ds(0, shards - 1)]
        arrived = pltpu.make_async_copy(others, others, recv_sems.at[phase])
        departed = pltpu.make_async_copy(others, others, send_sems.at[phase])
        return own, arrived, departed

    own_a, arrived_a, departed_a = exchange(send_a, recv_a, 0)

    for copy in loads[1:]:
        copy.wait()
    for i in range(4):
        owned[i] = jnp.concatenate([params[i], params[i]], axis=0).T
    owned[4] = jnp.broadcast_to(skip_ref[...], (2 * modes, chans)).T
    mine = pl.ds(me * per_dev, per_dev)
    decay, freq, real, imag, skip = [owned[i, mine, :] for i in range(5)]
    amplitude = 2.0 * jnp.sqrt(decay)
    real, imag = amplitude * real, amplitude * imag
    lanes = 2 * modes

    def is_imag(count):
        return lax.broadcasted_iota(jnp.int32, (count, lanes), 1) >= modes

    upper = is_imag(per_dev)
    step_real = jnp.exp(-decay) * jnp.cos(freq)
    step_imag = jnp.exp(-decay) * jnp.sin(freq)
    lead_real = real * step_real - imag * step_imag
    lead_imag = real * step_imag + imag * step_real
    lead_real = jnp.where(upper, -lead_real, lead_real)
    weights = jnp.where(upper, -imag, real)
    far_mag = jnp.exp(-decay * CHUNK)
    far_real = far_mag * jnp.cos(freq * CHUNK)
    far_imag = far_mag * jnp.sin(freq * CHUNK)
    far_imag = jnp.where(upper, -far_imag, far_imag)

    groups = CHUNK // 8
    ahead = lax.broadcasted_iota(jnp.int32, (8, lanes), 0).astype(jnp.float32)
    starts = 8.0 * lax.broadcasted_iota(jnp.int32, (groups, lanes), 0).astype(jnp.float32)
    row_id = lax.broadcasted_iota(jnp.int32, (CHUNK, CHUNK), 0)
    col_id = lax.broadcasted_iota(jnp.int32, (CHUNK, CHUNK), 1)
    causal = col_id >= row_id
    quarter = jnp.where(is_imag(8), 0.5 * math.pi, 0.0)

    for c in range(per_dev):
        d_row, f_row = decay[c : c + 1], freq[c : c + 1]
        inner = jnp.exp(-d_row * ahead) * jnp.cos(f_row * ahead - quarter)
        back = 7.0 - ahead
        inner_back = jnp.exp(-d_row * back) * jnp.cos(f_row * back - quarter)
        inner_turned = pltpu.roll(inner, modes, 1)
        inner_back_turned = pltpu.roll(inner_back, modes, 1)
        outer_mag = jnp.exp(-d_row * starts)
        outer_real = outer_mag * jnp.cos(f_row * starts)
        outer_imag = outer_mag * jnp.sin(f_row * starts)
        outer_imag = jnp.where(is_imag(groups), outer_imag, -outer_imag)
        forward, backward = [], []
        for g in range(groups):
            turn_r, turn_i = outer_real[g : g + 1], outer_imag[g : g + 1]
            forward.append(turn_r * inner + turn_i * inner_turned)
            back_r = outer_real[groups - 1 - g : groups - g]
            back_i = outer_imag[groups - 1 - g : groups - g]
            backward.append(back_r * inner_back + back_i * inner_back_turned)
        high, low = split(jnp.concatenate(forward, axis=0))
        out_high[c] = high
        out_low[c] = low
        taps = product(
            jnp.broadcast_to(weights[c : c + 1], (16, lanes)), high, low, NT
        )[0:1]
        spread = pltpu.roll(
            jnp.broadcast_to(taps, (CHUNK, CHUNK)), 0, 1, stride=1, stride_axis=0
        )
        high, low = split(jnp.where(causal, spread, 0.0))
        in_high[c, :, 0:CHUNK] = high
        in_low[c, :, 0:CHUNK] = low
        high, low = split(jnp.concatenate(backward, axis=0))
        in_high[c, :, CHUNK:] = high
        in_low[c, :, CHUNK:] = low

    own_a.wait()
    arrived_a.wait()

    strided = per_dev % 8 == 0

    def take(c):
        if strided:
            flat = recv_a.reshape(total * per_dev, CHUNK)
            return flat[pl.ds(c, total, stride=per_dev), :]
        return recv_a[:, :, c, :].reshape(total, CHUNK)

    def put(c, value):
        if strided:
            flat = send_b.reshape(total * per_dev, CHUNK)
            flat[pl.ds(c, total, stride=per_dev), :] = value
        else:
            send_b[:, :, c, :] = value.reshape(shards, parts, CHUNK)

    for c in range(per_dev):
        signal = take(c)
        both = product(signal, in_high[c], in_low[c], NN)
        near[c] = both[:, :CHUNK] + skip[c : c + 1] * signal
        ends = both[:, CHUNK:]
        ends_real[pl.ds(c * total, total), :] = ends
        ends_imag[pl.ds(c * total, total), :] = pltpu.roll(ends, modes, 1)

    state_r = jnp.zeros((per_dev, lanes), jnp.float32)
    state_i = jnp.zeros((per_dev, lanes), jnp.float32)

    def advance(shard, state):
        state_r, state_i = state
        for part in range(parts):
            at = pl.ds(shard * parts + part, per_dev, stride=total)
            carried[at, :] = lead_real * state_r - lead_imag * state_i
            next_r = far_real * state_r - far_imag * state_i + ends_real[at, :]
            state_i = far_real * state_i + far_imag * state_r + ends_imag[at, :]
            state_r = next_r
        return state_r, state_i

    if shards <= 16:
        for shard in range(shards):
            state_r, state_i = advance(shard, (state_r, state_i))
    else:
        lax.fori_loop(0, shards, advance, (state_r, state_i))

    total_sum = jnp.zeros((total, CHUNK), jnp.float32)
    total_square = jnp.zeros((total, CHUNK), jnp.float32)
    for c in range(per_dev):
        state = carried[pl.ds(c * total, total), :]
        value = near[c] + product(state, out_high[c], out_low[c], NT)
        total_sum = total_sum + value
        total_square = total_square + value * value
        put(c, value)

    for shard in range(shards):
        rows_of = slice(shard * parts, (shard + 1) * parts)
        sums_to[shard, 0:parts] = total_sum[rows_of]
        sums_to[shard, parts : 2 * parts] = total_square[rows_of]

    own_b, arrived_b, departed_b = exchange(send_b, recv_b, 1)
    sums_copies = []
    for side in range(1, halves_of_ch):
        for hop in range(shards - 1, -1, -1):
            target = lax.rem(me + hop, shards)
            sums_copies.append(
                pltpu.make_async_remote_copy(
                    src_ref=sums_to.at[target],
                    dst_ref=sums_from.at[side - 1, me],
                    send_sem=pair_sems.at[0],
                    recv_sem=pair_sems.at[1],
                    device_id={"seq": target, "ch": lax.rem(my_ch + side, halves_of_ch)},
                    device_id_type=MESH,
                )
            )
    for copy in sums_copies:
        copy.start()
    own_b.wait()
    arrived_b.wait()
    own_sums, own_squares, blocks = [], [], []
    for part in range(parts):
        block = jnp.concatenate([recv_b[i, part] for i in range(shards)], axis=0)
        blocks.append(block)
        own_sums.append(jnp.sum(block, axis=0, keepdims=True))
        own_squares.append(jnp.sum(block * block, axis=0, keepdims=True))
    sums = jnp.concatenate(own_sums + own_squares, axis=0)
    if sums_copies:
        pltpu.make_async_copy(sums_from, sums_from, pair_sems.at[1]).wait()
    for side in range(halves_of_ch - 1):
        for shard in range(shards):
            sums = sums + sums_from[side, shard]
    means = sums / (chans * halves_of_ch)
    for part in range(parts):
        token_mean = means[part : part + 1]
        token_var = means[parts + part : parts + part + 1] - token_mean * token_mean
        scaled = (blocks[part] - token_mean) * lax.rsqrt(token_var + 1e-05)
        out_ref[part * CHUNK : (part + 1) * CHUNK, :] = scaled.T
    departed_a.wait()
    departed_b.wait()
    if sums_copies:
        pltpu.make_async_copy(sums_from, sums_from, pair_sems.at[0]).wait()


def on_device(signal, decay_rate, frequency, coeff_real, coeff_imag, skip_weight, norm_gain):
    rows, chans = signal.shape
    shards = lax.axis_size("seq")
    halves_of_ch = lax.axis_size("ch")
    modes = decay_rate.shape[1]
    per_dev = chans // shards
    parts = rows // CHUNK
    total = parts * shards
    lanes = 2 * modes
    f32, bf16 = jnp.float32, jnp.bfloat16
    anywhere = pl.BlockSpec(memory_space=pl.ANY)
    vmem = pl.BlockSpec(memory_space=pltpu.VMEM)
    normed = pl.pallas_call(
        functools.partial(kernel_body, shards, halves_of_ch),
        out_shape=pltpu.VMEM((rows, chans), f32),
        in_specs=[anywhere] * 5 + [vmem],
        out_specs=vmem,
        scratch_shapes=[
            pltpu.VMEM((rows, chans), f32),
            pltpu.VMEM((4, modes, chans), f32),
            pltpu.VMEM((shards, rows // CHUNK, per_dev, CHUNK), f32),
            pltpu.VMEM((shards, rows // CHUNK, per_dev, CHUNK), f32),
            pltpu.VMEM((shards, rows // CHUNK, per_dev, CHUNK), f32),
            pltpu.VMEM((shards, rows // CHUNK, per_dev, CHUNK), f32),
            pltpu.VMEM((shards, 2 * parts, CHUNK), f32),
            pltpu.VMEM((max(halves_of_ch - 1, 1), shards, 2 * parts, CHUNK), f32),
            pltpu.VMEM((per_dev, CHUNK, CHUNK + lanes), bf16),
            pltpu.VMEM((per_dev, CHUNK, CHUNK + lanes), bf16),
            pltpu.VMEM((per_dev, CHUNK, lanes), bf16),
            pltpu.VMEM((per_dev, CHUNK, lanes), bf16),
            pltpu.VMEM((per_dev, total, CHUNK), f32),
            pltpu.VMEM((per_dev * total, lanes), f32),
            pltpu.VMEM((per_dev * total, lanes), f32),
            pltpu.VMEM((per_dev * total, lanes), f32),
            pltpu.VMEM((5, chans, lanes), f32),
            pltpu.SemaphoreType.DMA((5,)),
            pltpu.SemaphoreType.DMA((2,)),
            pltpu.SemaphoreType.DMA((2,)),
            pltpu.SemaphoreType.DMA((2,)),
            pltpu.SemaphoreType.DMA((2,)),
        ],
        compiler_params=pltpu.CompilerParams(collective_id=0, has_side_effects=True),
        name="modal_conv",
    )(
        signal,
        decay_rate.T,
        frequency.T,
        coeff_real.T,
        coeff_imag.T,
        skip_weight.reshape(1, chans),
    )
    return normed * norm_gain[None, :]


def solution(mesh):
    placed = (
        P("seq", "ch"),
        P("ch", None),
        P("ch", None),
        P("ch", None),
        P("ch", None),
        P("ch"),
        P("ch"),
    )
    return jax.shard_map(
        on_device, mesh=mesh, in_specs=placed, out_specs=P("seq", "ch"), check_vma=False
    )
```

```python
import functools
import math

import jax
import jax.numpy as jnp
from jax import lax
from jax.experimental import pallas as pl
from jax.experimental.pallas import tpu as pltpu
from jax.sharding import PartitionSpec as P

MESH = pl.DeviceIdType.MESH
CHUNK = 128
NT = (((1,), (1,)), ((), ()))
NN = (((1,), (0,)), ((), ()))


def split(value):
    high = value.astype(jnp.bfloat16)
    low = (value - high.astype(jnp.float32)).astype(jnp.bfloat16)
    return high, low


def product(value, high_w, low_w, dims):
    rows = value.shape[0]
    high = value.astype(jnp.bfloat16).astype(jnp.float32)
    both = jnp.concatenate([high, value - high], axis=0).astype(jnp.bfloat16)
    out = lax.dot_general(both, high_w, dims, preferred_element_type=jnp.float32)
    out = out + lax.dot_general(both, low_w, dims, preferred_element_type=jnp.float32)
    return out[:rows] + out[rows:]


def kernel_body(
    inner,
    outer,
    halves_of_ch,
    sig_hbm,
    decay_hbm,
    freq_hbm,
    real_hbm,
    imag_hbm,
    skip_ref,
    out_ref,
    x_ref,
    params,
    send_a,
    recv_a,
    send_b,
    recv_b,
    sums_to,
    sums_from,
    end_high,
    end_low,
    near_high,
    near_low,
    out_high,
    out_low,
    near,
    ends_real,
    ends_imag,
    carried,
    owned,
    plane_to,
    plane_from,
    load_sems,
    send_sems,
    recv_sems,
    own_sems,
    pair_sems,
    plane_sems,
):
    me = lax.axis_index("seq")
    my_ch = lax.axis_index("ch")
    rows, chans = x_ref.shape
    my_outer, my_inner = me // inner, lax.rem(me, inner)
    base = my_outer * inner
    per_dev = chans // inner
    modes = decay_hbm.shape[0]
    parts = rows // CHUNK
    total = inner * parts

    barrier = pltpu.get_barrier_semaphore()
    peers = []
    for hop in range(1, outer):
        peers.append((lax.rem(my_outer + hop, outer) * inner + my_inner, my_ch))
    for side in range(halves_of_ch):
        for hop in range(1 if side == 0 else 0, inner):
            peers.append(
                (base + lax.rem(my_inner + hop, inner), lax.rem(my_ch + side, halves_of_ch))
            )
    for seq, ch in peers:
        pl.semaphore_signal(
            barrier, inc=1, device_id={"seq": seq, "ch": ch}, device_id_type=MESH
        )

    loads = [pltpu.make_async_copy(sig_hbm, x_ref, load_sems.at[0])]
    for i, ref in enumerate((decay_hbm, freq_hbm, real_hbm, imag_hbm)):
        loads.append(pltpu.make_async_copy(ref, params.at[i], load_sems.at[i + 1]))
    for copy in loads:
        copy.start()
    loads[0].wait()
    turned = x_ref[...].T
    for i in range(inner):
        for part in range(parts):
            send_a[i, part] = turned[
                i * per_dev : (i + 1) * per_dev, part * CHUNK : (part + 1) * CHUNK
            ]

    def exchange(source, landing, phase):
        own = pltpu.make_async_copy(
            source.at[my_inner], landing.at[my_inner], own_sems.at[phase]
        )
        copies = []
        for hop in range(inner - 1, 0, -1):
            target = lax.rem(my_inner + hop, inner)
            copies.append(
                pltpu.make_async_remote_copy(
                    src_ref=source.at[target],
                    dst_ref=landing.at[my_inner],
                    send_sem=send_sems.at[phase],
                    recv_sem=recv_sems.at[phase],
                    device_id={"seq": base + target, "ch": my_ch},
                    device_id_type=MESH,
                )
            )
        for copy in copies:
            copy.start()
        own.start()
        others = landing.at[pl.ds(0, inner - 1)]
        arrived = pltpu.make_async_copy(others, others, recv_sems.at[phase])
        departed = pltpu.make_async_copy(others, others, send_sems.at[phase])
        return own, arrived, departed

    for copy in loads[1:]:
        copy.wait()
    for i in range(4):
        owned[i] = jnp.concatenate([params[i], params[i]], axis=0).T
    owned[4] = jnp.broadcast_to(skip_ref[...], (2 * modes, chans)).T
    mine = pl.ds(my_inner * per_dev, per_dev)
    decay, freq, real, imag, skip = [owned[i, mine, :] for i in range(5)]
    amplitude = 2.0 * jnp.sqrt(decay)
    real, imag = amplitude * real, amplitude * imag
    lanes = 2 * modes

    def is_imag(count):
        return lax.broadcasted_iota(jnp.int32, (count, lanes), 1) >= modes

    upper = is_imag(per_dev)
    step_real = jnp.exp(-decay) * jnp.cos(freq)
    step_imag = jnp.exp(-decay) * jnp.sin(freq)
    lead_real = real * step_real - imag * step_imag
    lead_imag = real * step_imag + imag * step_real
    lead_real = jnp.where(upper, -lead_real, lead_real)
    weights = jnp.where(upper, -imag, real)
    far_mag = jnp.exp(-decay * CHUNK)
    far_real = far_mag * jnp.cos(freq * CHUNK)
    far_imag = far_mag * jnp.sin(freq * CHUNK)
    far_imag = jnp.where(upper, -far_imag, far_imag)
    plane_mag = jnp.exp(-decay * (CHUNK * total))
    plane_real = plane_mag * jnp.cos(freq * (CHUNK * total))
    plane_imag = plane_mag * jnp.sin(freq * (CHUNK * total))
    plane_imag = jnp.where(upper, -plane_imag, plane_imag)

    groups = CHUNK // 8
    ahead = lax.broadcasted_iota(jnp.int32, (8, lanes), 0).astype(jnp.float32)
    starts = 8.0 * lax.broadcasted_iota(jnp.int32, (groups, lanes), 0).astype(jnp.float32)
    row_id = lax.broadcasted_iota(jnp.int32, (CHUNK, CHUNK), 0)
    col_id = lax.broadcasted_iota(jnp.int32, (CHUNK, CHUNK), 1)
    causal = col_id >= row_id
    quarter = jnp.where(is_imag(8), 0.5 * math.pi, 0.0)

    def build(c):
        d_row, f_row = decay[c : c + 1], freq[c : c + 1]
        inner = jnp.exp(-d_row * ahead) * jnp.cos(f_row * ahead - quarter)
        back = 7.0 - ahead
        inner_back = jnp.exp(-d_row * back) * jnp.cos(f_row * back - quarter)
        inner_turned = pltpu.roll(inner, modes, 1)
        inner_back_turned = pltpu.roll(inner_back, modes, 1)
        outer_mag = jnp.exp(-d_row * starts)
        outer_real = outer_mag * jnp.cos(f_row * starts)
        outer_imag = outer_mag * jnp.sin(f_row * starts)
        outer_imag = jnp.where(is_imag(groups), outer_imag, -outer_imag)
        forward, backward = [], []
        for g in range(groups):
            turn_r, turn_i = outer_real[g : g + 1], outer_imag[g : g + 1]
            forward.append(turn_r * inner + turn_i * inner_turned)
            back_r = outer_real[groups - 1 - g : groups - g]
            back_i = outer_imag[groups - 1 - g : groups - g]
            backward.append(back_r * inner_back + back_i * inner_back_turned)
        high, low = split(jnp.concatenate(forward, axis=0))
        out_high[c] = high
        out_low[c] = low
        taps = product(
            jnp.broadcast_to(weights[c : c + 1], (16, lanes)), high, low, NT
        )[0:1]
        spread = pltpu.roll(
            jnp.broadcast_to(taps, (CHUNK, CHUNK)), 0, 1, stride=1, stride_axis=0
        )
        high, low = split(jnp.where(causal, spread, 0.0))
        near_high[c] = high
        near_low[c] = low
        high, low = split(jnp.concatenate(backward, axis=0))
        end_high[c] = high
        end_low[c] = low

    for c in range(per_dev // 2):
        build(c)
    pl.semaphore_wait(barrier, len(peers))
    own_a, arrived_a, departed_a = exchange(send_a, recv_a, 0)
    for c in range(per_dev // 2, per_dev):
        build(c)

    own_a.wait()
    arrived_a.wait()

    strided = per_dev % 8 == 0

    def take(c):
        if strided:
            flat = recv_a.reshape(total * per_dev, CHUNK)
            return flat[pl.ds(c, total, stride=per_dev), :]
        return recv_a[:, :, c, :].reshape(total, CHUNK)

    def put(c, value):
        if strided:
            flat = send_b.reshape(total * per_dev, CHUNK)
            flat[pl.ds(c, total, stride=per_dev), :] = value
        else:
            send_b[:, :, c, :] = value.reshape(inner, parts, CHUNK)

    for c in range(per_dev):
        ends = product(take(c), end_high[c], end_low[c], NN)
        ends_real[pl.ds(c * total, total), :] = ends
        ends_imag[pl.ds(c * total, total), :] = pltpu.roll(ends, modes, 1)

    def advance(state_r, state_i, chunk, keep):
        at = pl.ds(chunk, per_dev, stride=total)
        if keep:
            carried[at, :] = lead_real * state_r - lead_imag * state_i
        next_r = far_real * state_r - far_imag * state_i + ends_real[at, :]
        next_i = far_real * state_i + far_imag * state_r + ends_imag[at, :]
        return next_r, next_i

    zero = jnp.zeros((per_dev, lanes), jnp.float32)
    state_r, state_i = zero, zero
    for chunk in range(total):
        state_r, state_i = advance(state_r, state_i, chunk, False)
    plane_to[...] = state_r
    plane_from[my_outer] = state_r
    plane_copies = []
    for hop in range(outer - 1, 0, -1):
        target = lax.rem(my_outer + hop, outer)
        plane_copies.append(
            pltpu.make_async_remote_copy(
                src_ref=plane_to,
                dst_ref=plane_from.at[my_outer],
                send_sem=plane_sems.at[0],
                recv_sem=plane_sems.at[1],
                device_id={"seq": target * inner + my_inner, "ch": my_ch},
                device_id_type=MESH,
            )
        )
    for copy in plane_copies:
        copy.start()

    for c in range(per_dev):
        signal = take(c)
        near[c] = product(signal, near_high[c], near_low[c], NN) + skip[c : c + 1] * signal

    others = plane_from.at[pl.ds(0, outer - 1)]
    pltpu.make_async_copy(others, others, plane_sems.at[1]).wait()
    state_r, state_i = zero, zero
    for plane in range(outer - 1):
        before = plane < my_outer
        left_r = plane_from[plane]
        left_i = pltpu.roll(left_r, modes, 1)
        next_r = plane_real * state_r - plane_imag * state_i + left_r
        next_i = plane_real * state_i + plane_imag * state_r + left_i
        state_r = jnp.where(before, next_r, state_r)
        state_i = jnp.where(before, next_i, state_i)
    for chunk in range(total):
        state_r, state_i = advance(state_r, state_i, chunk, True)

    total_sum = jnp.zeros((total, CHUNK), jnp.float32)
    total_square = jnp.zeros((total, CHUNK), jnp.float32)
    for c in range(per_dev):
        state = carried[pl.ds(c * total, total), :]
        value = near[c] + product(state, out_high[c], out_low[c], NT)
        total_sum = total_sum + value
        total_square = total_square + value * value
        put(c, value)

    for shard in range(inner):
        rows_of = slice(shard * parts, (shard + 1) * parts)
        sums_to[shard, 0:parts] = total_sum[rows_of]
        sums_to[shard, parts : 2 * parts] = total_square[rows_of]

    own_b, arrived_b, departed_b = exchange(send_b, recv_b, 1)
    sums_copies = []
    for side in range(1, halves_of_ch):
        for hop in range(inner - 1, -1, -1):
            target = lax.rem(my_inner + hop, inner)
            sums_copies.append(
                pltpu.make_async_remote_copy(
                    src_ref=sums_to.at[target],
                    dst_ref=sums_from.at[side - 1, my_inner],
                    send_sem=pair_sems.at[0],
                    recv_sem=pair_sems.at[1],
                    device_id={
                        "seq": base + target,
                        "ch": lax.rem(my_ch + side, halves_of_ch),
                    },
                    device_id_type=MESH,
                )
            )
    for copy in sums_copies:
        copy.start()
    own_b.wait()
    arrived_b.wait()
    own_sums, own_squares, blocks = [], [], []
    for part in range(parts):
        block = jnp.concatenate([recv_b[i, part] for i in range(inner)], axis=0)
        blocks.append(block)
        own_sums.append(jnp.sum(block, axis=0, keepdims=True))
        own_squares.append(jnp.sum(block * block, axis=0, keepdims=True))
    sums = jnp.concatenate(own_sums + own_squares, axis=0)
    if sums_copies:
        pltpu.make_async_copy(sums_from, sums_from, pair_sems.at[1]).wait()
    for side in range(halves_of_ch - 1):
        for shard in range(inner):
            sums = sums + sums_from[side, shard]
    means = sums / (chans * halves_of_ch)
    for part in range(parts):
        token_mean = means[part : part + 1]
        token_var = means[parts + part : parts + part + 1] - token_mean * token_mean
        scaled = (blocks[part] - token_mean) * lax.rsqrt(token_var + 1e-05)
        out_ref[part * CHUNK : (part + 1) * CHUNK, :] = scaled.T
    departed_a.wait()
    departed_b.wait()
    pltpu.make_async_copy(others, others, plane_sems.at[0]).wait()
    if sums_copies:
        pltpu.make_async_copy(sums_from, sums_from, pair_sems.at[0]).wait()


def on_device(signal, decay_rate, frequency, coeff_real, coeff_imag, skip_weight, norm_gain):
    rows, chans = signal.shape
    shards = lax.axis_size("seq")
    halves_of_ch = lax.axis_size("ch")
    modes = decay_rate.shape[1]
    inner = 1
    while (2 * inner) ** 2 <= shards:
        inner *= 2
    outer = shards // inner
    per_dev = chans // inner
    parts = rows // CHUNK
    total = parts * inner
    lanes = 2 * modes
    f32, bf16 = jnp.float32, jnp.bfloat16
    anywhere = pl.BlockSpec(memory_space=pl.ANY)
    vmem = pl.BlockSpec(memory_space=pltpu.VMEM)
    normed = pl.pallas_call(
        functools.partial(kernel_body, inner, outer, halves_of_ch),
        out_shape=pltpu.VMEM((rows, chans), f32),
        in_specs=[anywhere] * 5 + [vmem],
        out_specs=vmem,
        scratch_shapes=[
            pltpu.VMEM((rows, chans), f32),
            pltpu.VMEM((4, modes, chans), f32),
            pltpu.VMEM((inner, parts, per_dev, CHUNK), f32),
            pltpu.VMEM((inner, parts, per_dev, CHUNK), f32),
            pltpu.VMEM((inner, parts, per_dev, CHUNK), f32),
            pltpu.VMEM((inner, parts, per_dev, CHUNK), f32),
            pltpu.VMEM((inner, 2 * parts, CHUNK), f32),
            pltpu.VMEM((max(halves_of_ch - 1, 1), inner, 2 * parts, CHUNK), f32),
            pltpu.VMEM((per_dev, CHUNK, lanes), bf16),
            pltpu.VMEM((per_dev, CHUNK, lanes), bf16),
            pltpu.VMEM((per_dev, CHUNK, CHUNK), bf16),
            pltpu.VMEM((per_dev, CHUNK, CHUNK), bf16),
            pltpu.VMEM((per_dev, CHUNK, lanes), bf16),
            pltpu.VMEM((per_dev, CHUNK, lanes), bf16),
            pltpu.VMEM((per_dev, total, CHUNK), f32),
            pltpu.VMEM((per_dev * total, lanes), f32),
            pltpu.VMEM((per_dev * total, lanes), f32),
            pltpu.VMEM((per_dev * total, lanes), f32),
            pltpu.VMEM((5, chans, lanes), f32),
            pltpu.VMEM((per_dev, lanes), f32),
            pltpu.VMEM((outer, per_dev, lanes), f32),
            pltpu.SemaphoreType.DMA((5,)),
            pltpu.SemaphoreType.DMA((2,)),
            pltpu.SemaphoreType.DMA((2,)),
            pltpu.SemaphoreType.DMA((2,)),
            pltpu.SemaphoreType.DMA((2,)),
            pltpu.SemaphoreType.DMA((2,)),
        ],
        compiler_params=pltpu.CompilerParams(collective_id=0, has_side_effects=True),
        name="modal_conv",
    )(
        signal,
        decay_rate.T,
        frequency.T,
        coeff_real.T,
        coeff_imag.T,
        skip_weight.reshape(1, chans),
    )
    return normed * norm_gain[None, :]


def solution(mesh):
    placed = (
        P("seq", "ch"),
        P("ch", None),
        P("ch", None),
        P("ch", None),
        P("ch", None),
        P("ch"),
        P("ch"),
    )
    return jax.shard_map(
        on_device, mesh=mesh, in_specs=placed, out_specs=P("seq", "ch"), check_vma=False
    )
```

```python
import functools
import math

import jax
import jax.numpy as jnp
from jax import lax
from jax.experimental import pallas as pl
from jax.experimental.pallas import tpu as pltpu
from jax.sharding import PartitionSpec as P

MESH = pl.DeviceIdType.MESH
CHUNK = 128
NT = (((1,), (1,)), ((), ()))
NN = (((1,), (0,)), ((), ()))


def split(value):
    high = value.astype(jnp.bfloat16)
    low = (value - high.astype(jnp.float32)).astype(jnp.bfloat16)
    return high, low


def product(value, weights, dims):
    rows = value.shape[0]
    high = value.astype(jnp.bfloat16).astype(jnp.float32)
    both = jnp.concatenate([high, value - high], axis=0).astype(jnp.bfloat16)
    out = lax.dot_general(both, weights, dims, preferred_element_type=jnp.float32)
    width = out.shape[1] // 2
    return out[:rows, :width] + (out[rows:, :width] + out[:rows, width:])


def kernel_body(
    inner,
    outer,
    halves_of_ch,
    sig_hbm,
    decay_hbm,
    freq_hbm,
    real_hbm,
    imag_hbm,
    skip_ref,
    out_ref,
    x_ref,
    params,
    send_a,
    recv_a,
    send_b,
    recv_b,
    sums_to,
    sums_from,
    end_w,
    near_w,
    out_w,
    near,
    ends_real,
    ends_imag,
    carried,
    owned,
    plane_to,
    plane_from,
    load_sems,
    send_sems,
    recv_sems,
    own_sems,
    pair_sems,
    plane_sems,
):
    me = lax.axis_index("seq")
    my_ch = lax.axis_index("ch")
    rows, chans = x_ref.shape
    my_outer, my_inner = me // inner, lax.rem(me, inner)
    base = my_outer * inner
    per_dev = chans // inner
    modes = decay_hbm.shape[0]
    parts = rows // CHUNK
    total = inner * parts

    barrier = pltpu.get_barrier_semaphore()
    peers = []
    for hop in range(1, outer):
        peers.append((lax.rem(my_outer + hop, outer) * inner + my_inner, my_ch))
    for side in range(halves_of_ch):
        for hop in range(1 if side == 0 else 0, inner):
            peers.append(
                (base + lax.rem(my_inner + hop, inner), lax.rem(my_ch + side, halves_of_ch))
            )
    for seq, ch in peers:
        pl.semaphore_signal(
            barrier, inc=1, device_id={"seq": seq, "ch": ch}, device_id_type=MESH
        )

    loads = [pltpu.make_async_copy(sig_hbm, x_ref, load_sems.at[0])]
    for i, ref in enumerate((decay_hbm, freq_hbm, real_hbm, imag_hbm)):
        loads.append(pltpu.make_async_copy(ref, params.at[i], load_sems.at[i + 1]))
    for copy in loads:
        copy.start()
    loads[0].wait()
    turned = x_ref[...].T
    for i in range(inner):
        for part in range(parts):
            send_a[i, part] = turned[
                i * per_dev : (i + 1) * per_dev, part * CHUNK : (part + 1) * CHUNK
            ]

    def exchange(source, landing, phase):
        own = pltpu.make_async_copy(
            source.at[my_inner], landing.at[my_inner], own_sems.at[phase]
        )
        copies = []
        for hop in range(inner - 1, 0, -1):
            target = lax.rem(my_inner + hop, inner)
            copies.append(
                pltpu.make_async_remote_copy(
                    src_ref=source.at[target],
                    dst_ref=landing.at[my_inner],
                    send_sem=send_sems.at[phase],
                    recv_sem=recv_sems.at[phase],
                    device_id={"seq": base + target, "ch": my_ch},
                    device_id_type=MESH,
                )
            )
        for copy in copies:
            copy.start()
        own.start()
        others = landing.at[pl.ds(0, inner - 1)]
        arrived = pltpu.make_async_copy(others, others, recv_sems.at[phase])
        departed = pltpu.make_async_copy(others, others, send_sems.at[phase])
        return own, arrived, departed

    pl.semaphore_wait(barrier, len(peers))
    own_a, arrived_a, departed_a = exchange(send_a, recv_a, 0)
    for copy in loads[1:]:
        copy.wait()
    for i in range(4):
        owned[i] = jnp.concatenate([params[i], params[i]], axis=0).T
    owned[4] = jnp.broadcast_to(skip_ref[...], (2 * modes, chans)).T
    mine = pl.ds(my_inner * per_dev, per_dev)
    decay, freq, real, imag, skip = [owned[i, mine, :] for i in range(5)]
    amplitude = 2.0 * jnp.sqrt(decay)
    real, imag = amplitude * real, amplitude * imag
    lanes = 2 * modes

    def is_imag(count):
        return lax.broadcasted_iota(jnp.int32, (count, lanes), 1) >= modes

    upper = is_imag(per_dev)
    step_real = jnp.exp(-decay) * jnp.cos(freq)
    step_imag = jnp.exp(-decay) * jnp.sin(freq)
    lead_real = real * step_real - imag * step_imag
    lead_imag = real * step_imag + imag * step_real
    lead_real = jnp.where(upper, -lead_real, lead_real)
    weights = jnp.where(upper, -imag, real)
    far_mag = jnp.exp(-decay * CHUNK)
    far_real = far_mag * jnp.cos(freq * CHUNK)
    far_imag = far_mag * jnp.sin(freq * CHUNK)
    far_imag = jnp.where(upper, -far_imag, far_imag)
    plane_mag = jnp.exp(-decay * (CHUNK * total))
    plane_real = plane_mag * jnp.cos(freq * (CHUNK * total))
    plane_imag = plane_mag * jnp.sin(freq * (CHUNK * total))
    plane_imag = jnp.where(upper, -plane_imag, plane_imag)

    groups = CHUNK // 8
    ahead = lax.broadcasted_iota(jnp.int32, (8, lanes), 0).astype(jnp.float32)
    starts = 8.0 * lax.broadcasted_iota(jnp.int32, (groups, lanes), 0).astype(jnp.float32)
    row_id = lax.broadcasted_iota(jnp.int32, (CHUNK, CHUNK), 0)
    col_id = lax.broadcasted_iota(jnp.int32, (CHUNK, CHUNK), 1)
    causal = col_id >= row_id
    quarter = jnp.where(is_imag(8), 0.5 * math.pi, 0.0)

    def build(c):
        d_row, f_row = decay[c : c + 1], freq[c : c + 1]
        inner = jnp.exp(-d_row * ahead) * jnp.cos(f_row * ahead - quarter)
        back = 7.0 - ahead
        inner_back = jnp.exp(-d_row * back) * jnp.cos(f_row * back - quarter)
        inner_turned = pltpu.roll(inner, modes, 1)
        inner_back_turned = pltpu.roll(inner_back, modes, 1)
        outer_mag = jnp.exp(-d_row * starts)
        outer_real = outer_mag * jnp.cos(f_row * starts)
        outer_imag = outer_mag * jnp.sin(f_row * starts)
        outer_imag = jnp.where(is_imag(groups), outer_imag, -outer_imag)
        forward, backward = [], []
        for g in range(groups):
            turn_r, turn_i = outer_real[g : g + 1], outer_imag[g : g + 1]
            forward.append(turn_r * inner + turn_i * inner_turned)
            back_r = outer_real[groups - 1 - g : groups - g]
            back_i = outer_imag[groups - 1 - g : groups - g]
            backward.append(back_r * inner_back + back_i * inner_back_turned)
        high, low = split(jnp.concatenate(forward, axis=0))
        joined = jnp.concatenate([high, low], axis=0)
        out_w[c] = joined
        taps = product(
            jnp.broadcast_to(weights[c : c + 1], (8, lanes)), joined, NT
        )[0:1]
        spread = pltpu.roll(
            jnp.broadcast_to(taps, (CHUNK, CHUNK)), 0, 1, stride=1, stride_axis=0
        )
        high, low = split(jnp.where(causal, spread, 0.0))
        near_w[c] = jnp.concatenate([high, low], axis=1)
        high, low = split(jnp.concatenate(backward, axis=0))
        end_w[c] = jnp.concatenate([high, low], axis=1)

    for c in range(per_dev):
        build(c)

    own_a.wait()
    arrived_a.wait()

    strided = per_dev % 8 == 0

    def take(c):
        if strided:
            flat = recv_a.reshape(total * per_dev, CHUNK)
            return flat[pl.ds(c, total, stride=per_dev), :]
        return recv_a[:, :, c, :].reshape(total, CHUNK)

    def put(c, value):
        if strided:
            flat = send_b.reshape(total * per_dev, CHUNK)
            flat[pl.ds(c, total, stride=per_dev), :] = value
        else:
            send_b[:, :, c, :] = value.reshape(inner, parts, CHUNK)

    for c in range(per_dev):
        ends = product(take(c), end_w[c], NN)
        ends_real[pl.ds(c * total, total), :] = ends
        ends_imag[pl.ds(c * total, total), :] = pltpu.roll(ends, modes, 1)

    def advance(state_r, state_i, chunk, keep):
        at = pl.ds(chunk, per_dev, stride=total)
        if keep:
            carried[at, :] = lead_real * state_r - lead_imag * state_i
        next_r = far_real * state_r - far_imag * state_i + ends_real[at, :]
        next_i = far_real * state_i + far_imag * state_r + ends_imag[at, :]
        return next_r, next_i

    zero = jnp.zeros((per_dev, lanes), jnp.float32)
    state_r, state_i = zero, zero
    for chunk in range(total):
        state_r, state_i = advance(state_r, state_i, chunk, False)
    plane_to[...] = state_r
    plane_from[my_outer] = state_r
    plane_copies = []
    for hop in range(outer - 1, 0, -1):
        target = lax.rem(my_outer + hop, outer)
        plane_copies.append(
            pltpu.make_async_remote_copy(
                src_ref=plane_to,
                dst_ref=plane_from.at[my_outer],
                send_sem=plane_sems.at[0],
                recv_sem=plane_sems.at[1],
                device_id={"seq": target * inner + my_inner, "ch": my_ch},
                device_id_type=MESH,
            )
        )
    for copy in plane_copies:
        copy.start()

    for c in range(per_dev):
        signal = take(c)
        near[c] = product(signal, near_w[c], NN) + skip[c : c + 1] * signal

    others = plane_from.at[pl.ds(0, outer - 1)]
    pltpu.make_async_copy(others, others, plane_sems.at[1]).wait()
    state_r, state_i = zero, zero
    for plane in range(outer - 1):
        before = plane < my_outer
        left_r = plane_from[plane]
        left_i = pltpu.roll(left_r, modes, 1)
        next_r = plane_real * state_r - plane_imag * state_i + left_r
        next_i = plane_real * state_i + plane_imag * state_r + left_i
        state_r = jnp.where(before, next_r, state_r)
        state_i = jnp.where(before, next_i, state_i)
    for chunk in range(total):
        state_r, state_i = advance(state_r, state_i, chunk, True)

    total_sum = jnp.zeros((total, CHUNK), jnp.float32)
    total_square = jnp.zeros((total, CHUNK), jnp.float32)
    for c in range(per_dev):
        state = carried[pl.ds(c * total, total), :]
        value = near[c] + product(state, out_w[c], NT)
        total_sum = total_sum + value
        total_square = total_square + value * value
        put(c, value)

    for shard in range(inner):
        rows_of = slice(shard * parts, (shard + 1) * parts)
        sums_to[shard, 0:parts] = total_sum[rows_of]
        sums_to[shard, parts : 2 * parts] = total_square[rows_of]

    own_b, arrived_b, departed_b = exchange(send_b, recv_b, 1)
    sums_copies = []
    for side in range(1, halves_of_ch):
        for hop in range(inner - 1, -1, -1):
            target = lax.rem(my_inner + hop, inner)
            sums_copies.append(
                pltpu.make_async_remote_copy(
                    src_ref=sums_to.at[target],
                    dst_ref=sums_from.at[side - 1, my_inner],
                    send_sem=pair_sems.at[0],
                    recv_sem=pair_sems.at[1],
                    device_id={
                        "seq": base + target,
                        "ch": lax.rem(my_ch + side, halves_of_ch),
                    },
                    device_id_type=MESH,
                )
            )
    for copy in sums_copies:
        copy.start()
    own_b.wait()
    arrived_b.wait()
    own_sums, own_squares, blocks = [], [], []
    for part in range(parts):
        block = jnp.concatenate([recv_b[i, part] for i in range(inner)], axis=0)
        blocks.append(block)
        own_sums.append(jnp.sum(block, axis=0, keepdims=True))
        own_squares.append(jnp.sum(block * block, axis=0, keepdims=True))
    sums = jnp.concatenate(own_sums + own_squares, axis=0)
    if sums_copies:
        pltpu.make_async_copy(sums_from, sums_from, pair_sems.at[1]).wait()
    for side in range(halves_of_ch - 1):
        for shard in range(inner):
            sums = sums + sums_from[side, shard]
    means = sums / (chans * halves_of_ch)
    for part in range(parts):
        token_mean = means[part : part + 1]
        token_var = means[parts + part : parts + part + 1] - token_mean * token_mean
        scaled = (blocks[part] - token_mean) * lax.rsqrt(token_var + 1e-05)
        out_ref[part * CHUNK : (part + 1) * CHUNK, :] = scaled.T
    departed_a.wait()
    departed_b.wait()
    pltpu.make_async_copy(others, others, plane_sems.at[0]).wait()
    if sums_copies:
        pltpu.make_async_copy(sums_from, sums_from, pair_sems.at[0]).wait()


def on_device(signal, decay_rate, frequency, coeff_real, coeff_imag, skip_weight, norm_gain):
    rows, chans = signal.shape
    shards = lax.axis_size("seq")
    halves_of_ch = lax.axis_size("ch")
    modes = decay_rate.shape[1]
    inner = 1
    while (2 * inner) ** 2 <= shards:
        inner *= 2
    outer = shards // inner
    per_dev = chans // inner
    parts = rows // CHUNK
    total = parts * inner
    lanes = 2 * modes
    f32, bf16 = jnp.float32, jnp.bfloat16
    anywhere = pl.BlockSpec(memory_space=pl.ANY)
    vmem = pl.BlockSpec(memory_space=pltpu.VMEM)
    normed = pl.pallas_call(
        functools.partial(kernel_body, inner, outer, halves_of_ch),
        out_shape=pltpu.VMEM((rows, chans), f32),
        in_specs=[anywhere] * 5 + [vmem],
        out_specs=vmem,
        scratch_shapes=[
            pltpu.VMEM((rows, chans), f32),
            pltpu.VMEM((4, modes, chans), f32),
            pltpu.VMEM((inner, parts, per_dev, CHUNK), f32),
            pltpu.VMEM((inner, parts, per_dev, CHUNK), f32),
            pltpu.VMEM((inner, parts, per_dev, CHUNK), f32),
            pltpu.VMEM((inner, parts, per_dev, CHUNK), f32),
            pltpu.VMEM((inner, 2 * parts, CHUNK), f32),
            pltpu.VMEM((max(halves_of_ch - 1, 1), inner, 2 * parts, CHUNK), f32),
            pltpu.VMEM((per_dev, CHUNK, 2 * lanes), bf16),
            pltpu.VMEM((per_dev, CHUNK, 2 * CHUNK), bf16),
            pltpu.VMEM((per_dev, 2 * CHUNK, lanes), bf16),
            pltpu.VMEM((per_dev, total, CHUNK), f32),
            pltpu.VMEM((per_dev * total, lanes), f32),
            pltpu.VMEM((per_dev * total, lanes), f32),
            pltpu.VMEM((per_dev * total, lanes), f32),
            pltpu.VMEM((5, chans, lanes), f32),
            pltpu.VMEM((per_dev, lanes), f32),
            pltpu.VMEM((outer, per_dev, lanes), f32),
            pltpu.SemaphoreType.DMA((5,)),
            pltpu.SemaphoreType.DMA((2,)),
            pltpu.SemaphoreType.DMA((2,)),
            pltpu.SemaphoreType.DMA((2,)),
            pltpu.SemaphoreType.DMA((2,)),
            pltpu.SemaphoreType.DMA((2,)),
        ],
        compiler_params=pltpu.CompilerParams(collective_id=0, has_side_effects=True),
        name="modal_conv",
    )(
        signal,
        decay_rate.T,
        frequency.T,
        coeff_real.T,
        coeff_imag.T,
        skip_weight.reshape(1, chans),
    )
    return normed * norm_gain[None, :]


def solution(mesh):
    placed = (
        P("seq", "ch"),
        P("ch", None),
        P("ch", None),
        P("ch", None),
        P("ch", None),
        P("ch"),
        P("ch"),
    )
    return jax.shard_map(
        on_device, mesh=mesh, in_specs=placed, out_specs=P("seq", "ch"), check_vma=False
    )
```
